32 devices in a mesh: row: 8 (over y, x, core), col: 4 (over z).
Axes of the slice: x: 2, y: 2, z: 4, core: 2. Of those that a mesh axis runs over, the one named last changes fastest.
Arguments:
- pair: bfloat16 [384, 384, 128], P('row', 'col'), may hold values from -6 to 6
- token_mask: int32 [384], replicated, may hold values from 0 to 1, as said below
- gain: float32 [2, 128], replicated, may hold values from 0.25 to 1.75
- w_proj: bfloat16 [2, 128, 512], replicated, may hold values from -3 to 3
- w_bias: bfloat16 [2, 128, 4], replicated, may hold values from -0.5 to 0.5
- w_out: bfloat16 [2, 128, 128], replicated, may hold values from -0.5 to 0.5
Outputs:
- updated: bfloat16 [384, 384, 128], P('row', 'col')
The draws below stay inside these ranges and needn't reach their ends.
Inputs may be any that keep to these rules, and one draw needn't show every extreme that they name: `token_mask`: the tokens form 4 chains of 96 positions each; in each chain the first L positions are 1 and the rest 0, with 48 <= L < 96.
All inputs are finite; a program needn't handle non-finite values.
Results may differ from the reference program's by a relative error of at most 0.03.
The reference program's roundings to bfloat16 on the way count: a program that leaves them out, or rounds other values in their place, can miss the bound.
Values may be sent and summed in bfloat16 or wider, within the bound.
A program may use at most 128 MiB of HBM per device.

```python
import jax
import jax.numpy as jnp
from jax import lax

C = 128
HEADS = 4
HEAD_DIM = 32
N = 384


def draw_token_mask(key, part):
    chain_len = N // 4
    lengths = jax.random.randint(key, (4,), N // 8, chain_len)
    position = jnp.arange(N, dtype=jnp.int32)
    chain_id = position // chain_len
    offset = position % chain_len
    limits = jnp.sum(jnp.where(chain_id[:, None] == jnp.arange(4, dtype=jnp.int32)[None, :], lengths[None, :], 0), axis=1)
    return (offset < limits).astype(jnp.int32)


def draw_w_proj(key, part):
    inner = HEADS * HEAD_DIM
    shape = (2, C, 4 * inner)
    base = jnp.clip(jax.random.normal(key, shape, jnp.float32), -6.0, 6.0)
    return (base / jnp.sqrt(jnp.float32(C))).astype(jnp.bfloat16)


def shard_levels(stream_key, shape, cuts, smallest, largest):
    loudness = 1.0
    for axis_at, shards_of in cuts:
        steps = jax.random.uniform(jax.random.fold_in(jax.random.fold_in(stream_key, 6), axis_at), (shards_of,), jnp.float32, smallest / len(cuts), largest / len(cuts))
        loudness = loudness * jnp.repeat(jnp.exp(steps), shape[axis_at] // shards_of).reshape((-1,) + (1,) * (len(shape) - 1 - axis_at))
    return loudness


def scatter_about(key, shape, scale, bound, pieces=(), kind=jnp.bfloat16):
    level = shard_levels(key, shape, pieces, -0.22, 0.18) if pieces else 1.0
    values = jax.random.normal(key, shape, jnp.float32) * scale * level
    return jnp.minimum(jnp.maximum(values, -bound), bound).astype(kind)


def setup_inputs(seed: int = 0) -> dict:
    streams_of = jax.random.split(jax.random.key(seed), 7)
    return {
        "pair": scatter_about(streams_of[0], (N, N, C), 1.0, 6.0, ((0, 8), (1, 4))),
        "token_mask": draw_token_mask(jax.random.fold_in(streams_of[6], 71), 0),
        "gain": jnp.clip(1.0 + 0.15 * jax.random.normal(streams_of[2], (2, C), jnp.float32), 0.25, 1.75),
        "w_proj": draw_w_proj(jax.random.fold_in(streams_of[6], 71), 0),
        "w_bias": scatter_about(streams_of[4], (2, C, HEADS), C ** -0.5, 0.5),
        "w_out": scatter_about(streams_of[5], (2, HEADS * HEAD_DIM, C), (HEADS * HEAD_DIM) ** -0.5, 0.5),
    }


def layer_norm(tile, gain):
    values = tile.astype(jnp.float32)
    average = lax.optimization_barrier(jnp.mean(values, axis=-1, keepdims=True))
    centred = values - average
    variance = lax.optimization_barrier(jnp.mean(centred * centred, axis=-1, keepdims=True))
    return centred * lax.rsqrt(variance + 1e-05) * gain

def starting_node(pair, token_mask, gain, w_proj, w_bias, w_out):
    count = pair.shape[0]
    inner = HEADS * HEAD_DIM
    normed = layer_norm(pair, gain).astype(jnp.bfloat16)
    flattened = normed.reshape(count * count, pair.shape[2])
    projected = jnp.dot(flattened, w_proj, preferred_element_type=jnp.float32)
    shape_four = (count, count, HEADS, HEAD_DIM)
    queries = (projected[:, :inner] / jnp.sqrt(jnp.float32(HEAD_DIM))).astype(jnp.bfloat16).reshape(shape_four)
    keys_all = projected[:, inner:2 * inner].astype(jnp.bfloat16).reshape(shape_four)
    values_all = projected[:, 2 * inner:3 * inner].astype(jnp.bfloat16).reshape(shape_four)
    gate = jax.nn.sigmoid(projected[:, 3 * inner:])
    bias = jnp.dot(flattened, w_bias, preferred_element_type=jnp.float32).astype(jnp.bfloat16).reshape(count, count, HEADS)
    bias_moved = jnp.transpose(bias, (0, 2, 1)).astype(jnp.float32)

    def one_row(items):
        query_row, key_row, value_row = items
        scores = jnp.einsum('jhd,khd->jhk', query_row.astype(jnp.float32), key_row.astype(jnp.float32)) + bias_moved
        scores = jnp.where(token_mask[None, None, :] > 0, scores, -1000000000.0)
        highest = lax.optimization_barrier(jnp.max(scores, axis=-1, keepdims=True))
        weights = jnp.exp(scores - highest)
        total = lax.optimization_barrier(jnp.sum(weights, axis=-1))
        rounded = lax.optimization_barrier(weights.astype(jnp.bfloat16)).astype(jnp.float32)
        mixed = jnp.einsum('jhk,khd->jhd', rounded, value_row.astype(jnp.float32))
        return mixed / total[..., None]
    attended = lax.map(one_row, (queries, keys_all, values_all))
    gated = (gate * attended.reshape(count * count, inner)).astype(jnp.bfloat16)
    update = jnp.dot(gated, w_out, preferred_element_type=jnp.float32)
    return (pair.astype(jnp.float32) + update.reshape(count, count, -1)).astype(jnp.bfloat16)

def reference(pair, token_mask, gain, w_proj, w_bias, w_out):
    flipped = jnp.transpose(pair, (1, 0, 2))
    first = jnp.transpose(starting_node(flipped, token_mask, gain[0], w_proj[0], w_bias[0], w_out[0]), (1, 0, 2))
    return starting_node(first, token_mask, gain[1], w_proj[1], w_bias[1], w_out[1])
```

```python
import functools
import math

import jax
import jax.numpy as jnp
from jax import lax
from jax.experimental import pallas as pl
from jax.experimental.pallas import tpu as pltpu
from jax.sharding import PartitionSpec as P

HEADS = 4
HEAD_DIM = 32
INNER = HEADS * HEAD_DIM
LOG2E = 1.4426950408889634
NT = (((1,), (1,)), ((), ()))
TN = (((0,), (0,)), ((), ()))


def normalize(tile, gain):
    values = tile.astype(jnp.float32)
    average = jnp.mean(values, axis=-1, keepdims=True)
    centred = values - average
    variance = jnp.mean(centred * centred, axis=-1, keepdims=True)
    return (centred * lax.rsqrt(variance + 1e-05) * gain).astype(jnp.bfloat16)


def attend(x, bias_ref, gain_ref, w_qvg_ref, w_k_ref, w_out_ref):
    count = x.shape[0]
    normed = normalize(x, gain_ref[...])
    qvg = lax.dot_general(w_qvg_ref[...], normed, NT, preferred_element_type=jnp.float32)
    keys = jnp.dot(normed, w_k_ref[...], preferred_element_type=jnp.float32).astype(jnp.bfloat16)
    queries = (qvg[:INNER] * (LOG2E / math.sqrt(HEAD_DIM))).astype(jnp.bfloat16)
    values = qvg[INNER : 2 * INNER].astype(jnp.bfloat16)
    gate = jax.nn.sigmoid(qvg[2 * INNER :])
    ones = jnp.ones((16, count), jnp.bfloat16)
    pieces = []
    for head in range(HEADS):
        low, high = head * HEAD_DIM, (head + 1) * HEAD_DIM
        parts = [queries[low:high]]
        if head:
            parts.insert(0, jnp.zeros((low, count), jnp.bfloat16))
        if head < HEADS - 1:
            parts.append(jnp.zeros((INNER - high, count), jnp.bfloat16))
        padded = jnp.concatenate(parts, axis=0)
        scores = jnp.dot(keys, padded, preferred_element_type=jnp.float32) + bias_ref[head]
        highest = jnp.max(scores, axis=0, keepdims=True)
        weights = jnp.exp2(scores - highest).astype(jnp.bfloat16)
        extended = jnp.concatenate([values[low:high], ones], axis=0)
        mixed = jnp.dot(extended, weights, preferred_element_type=jnp.float32)
        pieces.append(mixed[:HEAD_DIM] * (1.0 / mixed[HEAD_DIM : HEAD_DIM + 1]))
    gated = (gate * jnp.concatenate(pieces, axis=0)).astype(jnp.bfloat16)
    update = lax.dot_general(gated, w_out_ref[...], TN, preferred_element_type=jnp.float32)
    return (x.astype(jnp.float32) + update).astype(jnp.bfloat16)


def attention_kernel(x_ref, bias_ref, gain_ref, w_qvg_ref, w_k_ref, w_out_ref, out_ref):
    out_ref[0] = attend(x_ref[0], bias_ref, gain_ref, w_qvg_ref, w_k_ref, w_out_ref)


def split_weights(w_proj):
    w_turned = jnp.transpose(w_proj)
    w_qvg = jnp.concatenate([w_turned[:INNER], w_turned[2 * INNER :]], axis=0)
    return w_qvg, w_proj[:, INNER : 2 * INNER]


def attention(x, bias, gain, w_proj, w_out):
    rows, count, channels = x.shape
    w_qvg, w_k = split_weights(w_proj)
    whole = lambda *shape: pl.BlockSpec(shape, lambda i: (0,) * len(shape))
    return pl.pallas_call(
        attention_kernel,
        out_shape=jax.ShapeDtypeStruct(x.shape, jnp.bfloat16),
        grid=(rows,),
        in_specs=[
            pl.BlockSpec((1, count, channels), lambda i: (i, 0, 0)),
            whole(HEADS, count, count),
            whole(1, channels),
            whole(3 * INNER, channels),
            whole(channels, INNER),
            whole(INNER, channels),
        ],
        out_specs=pl.BlockSpec((1, count, channels), lambda i: (i, 0, 0)),
    )(x, bias, gain[None], w_qvg, w_k, w_out)


def meet(peers):
    barrier = pltpu.get_barrier_semaphore()
    for peer in peers:
        pl.semaphore_signal(barrier, inc=1, device_id=peer, device_id_type=pl.DeviceIdType.MESH)
    pl.semaphore_wait(barrier, len(peers))


def remote(source, target, send_sem, recv_sem, peer):
    return pltpu.make_async_remote_copy(
        src_ref=source,
        dst_ref=target,
        send_sem=send_sem,
        recv_sem=recv_sem,
        device_id=peer,
        device_id_type=pl.DeviceIdType.MESH,
    )


def exchange_kernel(size, shifts, piece_of, place_of, x_ref, out_ref, send_sems, recv_sems, own_sem):
    rows, cols = size
    row, col = lax.axis_index("row"), lax.axis_index("col")
    to = [(lax.rem(row + dr, rows), lax.rem(col + dc, cols)) for dr, dc in shifts]
    meet(to)
    copies = []
    for at, peer in enumerate(to):
        copy = remote(
            piece_of(x_ref, *peer), place_of(out_ref, row, col), send_sems.at[at], recv_sems.at[at], peer
        )
        copy.start()
        copies.append(copy)
    own = pltpu.make_async_copy(piece_of(x_ref, row, col), place_of(out_ref, row, col), own_sem)
    own.start()
    own.wait()
    for at, (dr, dc) in enumerate(shifts):
        source = (lax.rem(row + rows - dr, rows), lax.rem(col + cols - dc, cols))
        remote(
            piece_of(x_ref, row, col), place_of(out_ref, *source), send_sems.at[at], recv_sems.at[at], to[at]
        ).wait_recv()
    for copy in copies:
        copy.wait_send()


def exchange(x, out_shape, size, axes, piece_of, place_of, collective_id):
    shifts = shifts_of(size, axes)
    return pl.pallas_call(
        functools.partial(exchange_kernel, size, shifts, piece_of, place_of),
        out_shape=jax.ShapeDtypeStruct(out_shape, x.dtype),
        in_specs=[pl.BlockSpec(memory_space=pltpu.VMEM)],
        out_specs=pl.BlockSpec(memory_space=pltpu.VMEM),
        scratch_shapes=[
            pltpu.SemaphoreType.DMA((len(shifts),)),
            pltpu.SemaphoreType.DMA((len(shifts),)),
            pltpu.SemaphoreType.DMA,
        ],
        compiler_params=pltpu.CompilerParams(collective_id=collective_id, has_side_effects=True),
    )(x)


def gather_peers(size):
    rows, cols = size
    row, col = lax.axis_index("row"), lax.axis_index("col")
    in_col = [(row, lax.rem(col + d, cols)) for d in range(1, cols)]
    in_row = [(lax.rem(row + 2 * d, rows), col) for d in range(1, rows // 2)]
    partner = (row // 2 * 2 + 1 - lax.rem(row, 2), col)
    return in_col, in_row, partner


def gather_stages(size, part_ref, full_ref, send_sems, recv_sems, own_sem):
    rows, cols = size
    row, col = lax.axis_index("row"), lax.axis_index("col")
    half, core = row // 2, lax.rem(row, 2)
    in_col, in_row, partner = gather_peers(size)
    sent = []

    def send(source, target, at, peer):
        copy = remote(source, target, send_sems.at[at], recv_sems.at[at], peer)
        copy.start()
        sent.append(copy)

    def arrive(target, at, peer):
        remote(target, target, send_sems.at[at], recv_sems.at[at], peer).wait_recv()

    mine = full_ref.at[core, half, col]
    for at, peer in enumerate(in_col):
        send(part_ref, mine, at, peer)
    own = pltpu.make_async_copy(part_ref, mine, own_sem)
    own.start()
    own.wait()
    for at, peer in enumerate(in_col):
        arrive(full_ref.at[core, half, lax.rem(col + cols - at - 1, cols)], at, peer)
    base = len(in_col)
    for at, peer in enumerate(in_row):
        send(full_ref.at[core, half], full_ref.at[core, half], base + at, peer)
    halves = rows // 2
    for at, peer in enumerate(in_row):
        arrive(full_ref.at[core, lax.rem(half + halves - at - 1, halves)], base + at, peer)
    base += len(in_row)
    send(full_ref.at[core], full_ref.at[core], base, partner)
    arrive(full_ref.at[1 - core], base, partner)
    for copy in sent:
        copy.wait_send()


def gather_kernel(size, part_ref, full_ref, send_sems, recv_sems, own_sem):
    in_col, in_row, partner = gather_peers(size)
    meet(in_col + in_row + [partner])
    gather_stages(size, part_ref, full_ref, send_sems, recv_sems, own_sem)


def fused_kernel(
    size, shifts, piece_of, place_of, bias_too, x_ref, bias_ref, gain_ref, w_qvg_ref, w_k_ref, w_out_ref, *rest
):
    if bias_too:
        next_gain_ref, w_bias_ref, out_ref, full_ref, stage, send_sems, recv_sems, own_sem = rest[:8]
        part, gather_send, gather_recv, gather_own = rest[8:]
    else:
        out_ref, stage, send_sems, recv_sems, own_sem = rest
    width = x_ref.shape[0]
    rows, cols = size
    row, col = lax.axis_index("row"), lax.axis_index("col")
    to = [(lax.rem(row + dr, rows), lax.rem(col + dc, cols)) for dr, dc in shifts]
    meet(to)

    def push(at):
        one = pl.ds(at, 1)
        for index, peer in enumerate(to):
            remote(
                piece_of(stage, one, *peer),
                place_of(out_ref, one, row, col),
                send_sems.at[index],
                recv_sems.at[index],
                peer,
            ).start()
        pltpu.make_async_copy(piece_of(stage, one, row, col), place_of(out_ref, one, row, col), own_sem).start()

    def step(at, carry):
        @pl.when(at > 0)
        def _():
            push(at - 1)

        result = attend(x_ref[at], bias_ref, gain_ref, w_qvg_ref, w_k_ref, w_out_ref)
        stage[at] = result.reshape(stage.shape[1:])
        if bias_too:
            turned = lax.dot_general(
                w_bias_ref[...], normalize(result, next_gain_ref[...]), NT, preferred_element_type=jnp.float32
            )
            part[at] = turned[:HEADS].astype(jnp.bfloat16)
        return carry

    lax.fori_loop(0, width, step, 0)
    push(width - 1)
    if bias_too:
        gather_stages(size, part, full_ref, gather_send, gather_recv, gather_own)
    every = pl.ds(0, width)
    mine = piece_of(stage, every, row, col)
    pltpu.make_async_copy(mine, place_of(out_ref, every, row, col), own_sem).wait()
    for index, (dr, dc) in enumerate(shifts):
        source = (lax.rem(row + rows - dr, rows), lax.rem(col + cols - dc, cols))
        remote(
            mine, place_of(out_ref, every, *source), send_sems.at[index], recv_sems.at[index], to[index]
        ).wait_recv()
    for index, peer in enumerate(to):
        remote(
            piece_of(stage, every, *peer), place_of(out_ref, every, row, col), send_sems.at[index], recv_sems.at[index], peer
        ).wait_send()


def shifts_of(size, axes):
    return [
        (dr, dc)
        for dc in (range(size[1]) if "col" in axes else (0,))
        for dr in (range(size[0]) if "row" in axes else (0,))
        if dr or dc
    ]


def fused(x, bias, gain, w_proj, w_out, out_shape, stage_shape, size, axes, piece_of, place_of, collective_id, following=None):
    shifts = shifts_of(size, axes)
    operands = [x, bias, gain[None], *split_weights(w_proj), w_out]
    outs = [jax.ShapeDtypeStruct(out_shape, x.dtype)]
    scratch = [
        pltpu.VMEM(stage_shape, x.dtype),
        pltpu.SemaphoreType.DMA((len(shifts),)),
        pltpu.SemaphoreType.DMA((len(shifts),)),
        pltpu.SemaphoreType.DMA,
    ]
    if following is not None:
        next_gain, w_bias = following
        operands += [next_gain[None], jnp.pad(jnp.transpose(w_bias), ((0, 16 - HEADS), (0, 0)))]
        part_shape = (x.shape[0], HEADS, x.shape[1])
        outs.append(jax.ShapeDtypeStruct((2, size[0] // 2, size[1]) + part_shape, x.dtype))
        count = size[1] - 1 + size[0] // 2
        scratch += [
            pltpu.VMEM(part_shape, x.dtype),
            pltpu.SemaphoreType.DMA((count,)),
            pltpu.SemaphoreType.DMA((count,)),
            pltpu.SemaphoreType.DMA,
        ]
    return pl.pallas_call(
        functools.partial(fused_kernel, size, shifts, piece_of, place_of, following is not None),
        out_shape=outs,
        in_specs=[pl.BlockSpec(memory_space=pltpu.VMEM)] * len(operands),
        out_specs=[pl.BlockSpec(memory_space=pltpu.VMEM)] * len(outs),
        scratch_shapes=scratch,
        compiler_params=pltpu.CompilerParams(collective_id=collective_id, has_side_effects=True),
    )(*operands)


def gather(part, size, collective_id):
    count = size[1] - 1 + size[0] // 2 - 1 + 1
    return pl.pallas_call(
        functools.partial(gather_kernel, size),
        out_shape=jax.ShapeDtypeStruct((2, size[0] // 2, size[1]) + part.shape, part.dtype),
        in_specs=[pl.BlockSpec(memory_space=pltpu.VMEM)],
        out_specs=pl.BlockSpec(memory_space=pltpu.VMEM),
        scratch_shapes=[
            pltpu.SemaphoreType.DMA((count,)),
            pltpu.SemaphoreType.DMA((count,)),
            pltpu.SemaphoreType.DMA,
        ],
        compiler_params=pltpu.CompilerParams(collective_id=collective_id, has_side_effects=True),
    )(part)


def gather_bias(x, token_mask, gain, w_bias, size, ending):
    rows, count, channels = x.shape
    normed = normalize(x, gain)
    part = jnp.einsum("ikc,ch->ihk", normed, w_bias, preferred_element_type=jnp.float32)
    full = gather(part.astype(jnp.bfloat16), size, 0 if ending else 1)
    order = (4, 5, 2, 1, 0, 3) if ending else (4, 5, 1, 0, 2, 3)
    turned = jnp.transpose(full, order).reshape(HEADS, count, count).astype(jnp.float32) * LOG2E
    return jnp.where(token_mask[None, :, None] > 0, turned, -1000000000.0)


def swap(x, size):
    width, count, channels = x.shape
    rows, cols = size
    if width % 2:
        x = lax.all_to_all(x, "row", 1, 0, tiled=True)
        return lax.all_to_all(jnp.transpose(x, (1, 0, 2)), "col", 0, 1, tiled=True)
    pairs = width // 2
    moved = exchange(
        x.reshape(width, count // 2, 2, channels),
        (cols, rows, width, pairs, 2, channels),
        size,
        ("row", "col"),
        lambda ref, r, c: ref.at[:, pl.ds((r * cols + c) * pairs, pairs)],
        lambda ref, r, c: ref.at[c, r],
        3,
    )
    return jnp.transpose(moved.reshape(count, width, channels), (1, 0, 2))


def local(pair, token_mask, gain, w_proj, w_bias, w_out, size):
    rows, cols = size
    deep, wide, channels = pair.shape
    width, count = wide // rows, deep * rows
    flipped = jnp.transpose(pair, (1, 0, 2))
    x = exchange(
        flipped,
        (width, count, channels),
        size,
        ("row",),
        lambda ref, r, c: ref.at[pl.ds(r * width, width)],
        lambda ref, r, c: ref.at[:, pl.ds(pl.multiple_of(r * deep, deep), deep)],
        2,
    )
    bias = gather_bias(x, token_mask, gain[0], w_bias[0], size, True)
    if width % 2:
        x = attention(x, bias, gain[0], w_proj[0], w_out[0])
        x = swap(x, size)
        bias = gather_bias(x, token_mask, gain[1], w_bias[1], size, False)
    else:
        pairs = width // 2
        moved, full = fused(
            x,
            bias,
            gain[0],
            w_proj[0],
            w_out[0],
            (cols, rows, width, pairs, 2, channels),
            (width, count // 2, 2, channels),
            size,
            ("row", "col"),
            lambda ref, at, r, c: ref.at[at, pl.ds((r * cols + c) * pairs, pairs)],
            lambda ref, at, r, c: ref.at[c, r, at],
            3,
            (gain[1], w_bias[1]),
        )
        x = jnp.transpose(moved.reshape(count, width, channels), (1, 0, 2))
        turned = jnp.transpose(full, (4, 2, 1, 0, 3, 5)).reshape(HEADS, count, count)
        bias = jnp.where(token_mask[None, :, None] > 0, turned.astype(jnp.float32) * LOG2E, -1000000000.0)
    return fused(
        x,
        bias,
        gain[1],
        w_proj[1],
        w_out[1],
        pair.shape,
        x.shape,
        size,
        ("col",),
        lambda ref, at, r, c: ref.at[at, pl.ds(pl.multiple_of(c * wide, wide), wide)],
        lambda ref, at, r, c: ref.at[pl.ds(c * width + at.start, at.size)],
        4,
    )[0]


def solution(mesh):
    size = (mesh.shape["row"], mesh.shape["col"])
    return jax.shard_map(
        functools.partial(local, size=size),
        mesh=mesh,
        in_specs=(P("row", "col", None), P(), P(), P(), P(), P()),
        out_specs=P("row", "col", None),
        check_vma=False,
    )
```

```python
import functools
import math

import jax
import jax.numpy as jnp
from jax import lax
from jax.experimental import pallas as pl
from jax.experimental.pallas import tpu as pltpu
from jax.sharding import PartitionSpec as P

HEADS = 4
HEAD_DIM = 32
INNER = HEADS * HEAD_DIM
LOG2E = 1.4426950408889634
NT = (((1,), (1,)), ((), ()))
TN = (((0,), (0,)), ((), ()))


def normalize(tile, gain):
    values = tile.astype(jnp.float32)
    average = jnp.mean(values, axis=-1, keepdims=True)
    centred = values - average
    variance = jnp.mean(centred * centred, axis=-1, keepdims=True)
    return (centred * lax.rsqrt(variance + 1e-05) * gain).astype(jnp.bfloat16)


def attend(x, bias_ref, gain, w_turned_ref, w_k, w_out):
    count = x.shape[0]
    normed = normalize(x, gain)
    queries = lax.dot_general(w_turned_ref[:INNER], normed, NT, preferred_element_type=jnp.float32)
    rest = lax.dot_general(w_turned_ref[2 * INNER :], normed, NT, preferred_element_type=jnp.float32)
    keys = jnp.dot(normed, w_k, preferred_element_type=jnp.float32).astype(jnp.bfloat16)
    queries = (queries * (LOG2E / math.sqrt(HEAD_DIM))).astype(jnp.bfloat16)
    values = rest[:INNER].astype(jnp.bfloat16)
    gate = jax.nn.sigmoid(rest[INNER:])
    ones = jnp.ones((16, count), jnp.bfloat16)
    pieces = []
    for head in range(HEADS):
        low, high = head * HEAD_DIM, (head + 1) * HEAD_DIM
        parts = [queries[low:high]]
        if head:
            parts.insert(0, jnp.zeros((low, count), jnp.bfloat16))
        if head < HEADS - 1:
            parts.append(jnp.zeros((INNER - high, count), jnp.bfloat16))
        padded = jnp.concatenate(parts, axis=0)
        scores = jnp.dot(keys, padded, preferred_element_type=jnp.float32) + bias_ref[head]
        highest = jnp.max(scores, axis=0, keepdims=True)
        weights = jnp.exp2(scores - highest).astype(jnp.bfloat16)
        extended = jnp.concatenate([values[low:high], ones], axis=0)
        mixed = jnp.dot(extended, weights, preferred_element_type=jnp.float32)
        pieces.append(mixed[:HEAD_DIM] * (1.0 / mixed[HEAD_DIM : HEAD_DIM + 1]))
    gated = (gate * jnp.concatenate(pieces, axis=0)).astype(jnp.bfloat16)
    update = lax.dot_general(gated, w_out, TN, preferred_element_type=jnp.float32)
    return (x.astype(jnp.float32) + update).astype(jnp.bfloat16)


def attention_kernel(x_ref, bias_ref, gain_ref, w_turned_ref, w_k_ref, w_out_ref, out_ref):
    out_ref[0] = attend(x_ref[0], bias_ref, gain_ref[...], w_turned_ref, w_k_ref[...], w_out_ref[...])


def attention(x, bias, gain, w_proj, w_out):
    rows, count, channels = x.shape
    whole = lambda *shape: pl.BlockSpec(shape, lambda i: (0,) * len(shape))
    return pl.pallas_call(
        attention_kernel,
        out_shape=jax.ShapeDtypeStruct(x.shape, jnp.bfloat16),
        grid=(rows,),
        in_specs=[
            pl.BlockSpec((1, count, channels), lambda i: (i, 0, 0)),
            whole(HEADS, count, count),
            whole(1, channels),
            whole(4 * INNER, channels),
            whole(channels, INNER),
            whole(INNER, channels),
        ],
        out_specs=pl.BlockSpec((1, count, channels), lambda i: (i, 0, 0)),
    )(x, bias, gain[None], jnp.transpose(w_proj), w_proj[:, INNER : 2 * INNER], w_out)


def meet(peers):
    barrier = pltpu.get_barrier_semaphore()
    for peer in peers:
        pl.semaphore_signal(barrier, inc=1, device_id=peer, device_id_type=pl.DeviceIdType.MESH)
    pl.semaphore_wait(barrier, len(peers))


def remote(source, target, send_sem, recv_sem, peer):
    return pltpu.make_async_remote_copy(
        src_ref=source,
        dst_ref=target,
        send_sem=send_sem,
        recv_sem=recv_sem,
        device_id=peer,
        device_id_type=pl.DeviceIdType.MESH,
    )


def gather_peers(size):
    rows, cols = size
    row, col = lax.axis_index("row"), lax.axis_index("col")
    in_col = [(row, lax.rem(col + d, cols)) for d in range(1, cols)]
    in_row = [(lax.rem(row + 2 * d, rows), col) for d in range(1, rows // 2)]
    partner = (row // 2 * 2 + 1 - lax.rem(row, 2), col)
    return in_col, in_row, partner


def gather_stages(size, part_ref, full_ref, send_sems, recv_sems, own_sem):
    rows, cols = size
    row, col = lax.axis_index("row"), lax.axis_index("col")
    half, core = row // 2, lax.rem(row, 2)
    in_col, in_row, partner = gather_peers(size)
    sent = []

    def send(source, target, at, peer):
        copy = remote(source, target, send_sems.at[at], recv_sems.at[at], peer)
        copy.start()
        sent.append(copy)

    def arrive(target, at, peer):
        remote(target, target, send_sems.at[at], recv_sems.at[at], peer).wait_recv()

    mine = full_ref.at[core, half, col]
    for at, peer in enumerate(in_col):
        send(part_ref, mine, at, peer)
    own = pltpu.make_async_copy(part_ref, mine, own_sem)
    own.start()
    own.wait()
    for at, peer in enumerate(in_col):
        arrive(full_ref.at[core, half, lax.rem(col + cols - at - 1, cols)], at, peer)
    base = len(in_col)
    for at, peer in enumerate(in_row):
        send(full_ref.at[core, half], full_ref.at[core, half], base + at, peer)
    halves = rows // 2
    for at, peer in enumerate(in_row):
        arrive(full_ref.at[core, lax.rem(half + halves - at - 1, halves)], base + at, peer)
    base += len(in_row)
    send(full_ref.at[core], full_ref.at[core], base, partner)
    arrive(full_ref.at[1 - core], base, partner)
    for copy in sent:
        copy.wait_send()


def gather_kernel(size, part_ref, full_ref, send_sems, recv_sems, own_sem):
    in_col, in_row, partner = gather_peers(size)
    meet(in_col + in_row + [partner])
    gather_stages(size, part_ref, full_ref, send_sems, recv_sems, own_sem)


def fused_kernel(
    size, shifts, piece_of, place_of, turn, x_ref, bias_ref, gain_ref, w_proj_ref, w_bias_ref, w_out_ref, *rest
):
    bias_too = turn == 0
    if bias_too:
        out_ref, full_ref, stage, turned_ref, send_sems, recv_sems, own_sem = rest[:7]
        part, gather_send, gather_recv, gather_own = rest[7:]
    else:
        out_ref, stage, turned_ref, send_sems, recv_sems, own_sem = rest
    width = x_ref.shape[0]
    rows, cols = size
    row, col = lax.axis_index("row"), lax.axis_index("col")
    to = [(lax.rem(row + dr, rows), lax.rem(col + dc, cols)) for dr, dc in shifts]
    meet(to)
    turned_ref[...] = jnp.transpose(w_proj_ref[turn].astype(jnp.float32)).astype(jnp.bfloat16)

    def push(at):
        one = pl.ds(at, 1)
        for index, peer in enumerate(to):
            remote(
                piece_of(stage, one, *peer),
                place_of(out_ref, one, row, col),
                send_sems.at[index],
                recv_sems.at[index],
                peer,
            ).start()
        pltpu.make_async_copy(piece_of(stage, one, row, col), place_of(out_ref, one, row, col), own_sem).start()

    def step(at, carry):
        @pl.when(at > 0)
        def _():
            push(at - 1)

        result = attend(
            x_ref[at],
            bias_ref,
            gain_ref[turn : turn + 1],
            turned_ref,
            w_proj_ref[turn, :, INNER : 2 * INNER],
            w_out_ref[turn],
        )
        stage[at] = result.reshape(stage.shape[1:])
        if bias_too:
            turned = lax.dot_general(
                w_bias_ref[1], normalize(result, gain_ref[1:2]), NT, preferred_element_type=jnp.float32
            )
            part[at] = turned[:HEADS].astype(jnp.bfloat16)
        return carry

    lax.fori_loop(0, width, step, 0)
    push(width - 1)
    if bias_too:
        gather_stages(size, part, full_ref, gather_send, gather_recv, gather_own)
    every = pl.ds(0, width)
    mine = piece_of(stage, every, row, col)
    pltpu.make_async_copy(mine, place_of(out_ref, every, row, col), own_sem).wait()
    for index, (dr, dc) in enumerate(shifts):
        source = (lax.rem(row + rows - dr, rows), lax.rem(col + cols - dc, cols))
        remote(
            mine, place_of(out_ref, every, *source), send_sems.at[index], recv_sems.at[index], to[index]
        ).wait_recv()
    for index, peer in enumerate(to):
        remote(
            piece_of(stage, every, *peer), place_of(out_ref, every, row, col), send_sems.at[index], recv_sems.at[index], peer
        ).wait_send()


def shifts_of(size, axes):
    return [
        (dr, dc)
        for dc in (range(size[1]) if "col" in axes else (0,))
        for dr in (range(size[0]) if "row" in axes else (0,))
        if dr or dc
    ]


def fused(x, bias, gain, w_proj, w_bias, w_out, turn, out_shape, stage_shape, size, axes, piece_of, place_of, collective_id):
    shifts = shifts_of(size, axes)
    operands = [x, bias, gain, w_proj, w_bias, w_out]
    outs = [jax.ShapeDtypeStruct(out_shape, x.dtype)]
    scratch = [
        pltpu.VMEM(stage_shape, x.dtype),
        pltpu.VMEM((w_proj.shape[2], w_proj.shape[1]), x.dtype),
        pltpu.SemaphoreType.DMA((len(shifts),)),
        pltpu.SemaphoreType.DMA((len(shifts),)),
        pltpu.SemaphoreType.DMA,
    ]
    if turn == 0:
        part_shape = (x.shape[0], HEADS, x.shape[1])
        outs.append(jax.ShapeDtypeStruct((2, size[0] // 2, size[1]) + part_shape, x.dtype))
        count = size[1] - 1 + size[0] // 2
        scratch += [
            pltpu.VMEM(part_shape, x.dtype),
            pltpu.SemaphoreType.DMA((count,)),
            pltpu.SemaphoreType.DMA((count,)),
            pltpu.SemaphoreType.DMA,
        ]
    return pl.pallas_call(
        functools.partial(fused_kernel, size, shifts, piece_of, place_of, turn),
        out_shape=outs,
        in_specs=[pl.BlockSpec(memory_space=pltpu.VMEM)] * len(operands),
        out_specs=[pl.BlockSpec(memory_space=pltpu.VMEM)] * len(outs),
        scratch_shapes=scratch,
        compiler_params=pltpu.CompilerParams(collective_id=collective_id, has_side_effects=True),
    )(*operands)


def gather(part, size, collective_id):
    count = size[1] - 1 + size[0] // 2 - 1 + 1
    return pl.pallas_call(
        functools.partial(gather_kernel, size),
        out_shape=jax.ShapeDtypeStruct((2, size[0] // 2, size[1]) + part.shape, part.dtype),
        in_specs=[pl.BlockSpec(memory_space=pltpu.VMEM)],
        out_specs=pl.BlockSpec(memory_space=pltpu.VMEM),
        scratch_shapes=[
            pltpu.SemaphoreType.DMA((count,)),
            pltpu.SemaphoreType.DMA((count,)),
            pltpu.SemaphoreType.DMA,
        ],
        compiler_params=pltpu.CompilerParams(collective_id=collective_id, has_side_effects=True),
    )(part)


def gather_bias(x, token_mask, gain, w_bias, size):
    rows, count, channels = x.shape
    normed = normalize(x, gain)
    part = jnp.einsum("ikc,ch->ihk", normed, w_bias, preferred_element_type=jnp.float32)
    full = gather(part.astype(jnp.bfloat16), size, 1)
    turned = jnp.transpose(full, (4, 5, 1, 0, 2, 3)).reshape(HEADS, count, count)
    return finish_bias(turned, token_mask)


def finish_bias(turned, token_mask):
    return jnp.where(token_mask[None, :, None] > 0, turned.astype(jnp.float32) * LOG2E, -1000000000.0)


def swap(x, size):
    width, count, channels = x.shape
    rows, cols = size
    x = lax.all_to_all(x, "row", 1, 0, tiled=True)
    return lax.all_to_all(jnp.transpose(x, (1, 0, 2)), "col", 0, 1, tiled=True)


def entry_kernel(
    size, shifts, piece_of, place_of, pair_ref, flipped_ref, gain_ref, w_bias_ref, x_ref, full_ref, part,
    send_sems, recv_sems, own_sem, gather_send, gather_recv, gather_own
):
    rows, cols = size
    row, col = lax.axis_index("row"), lax.axis_index("col")
    to = [(lax.rem(row + dr, rows), col) for dr, dc in shifts]
    in_col, in_row, partner = gather_peers(size)
    meet(to + in_col)
    copies = [
        remote(piece_of(flipped_ref, *peer), place_of(x_ref, row, col), send_sems.at[at], recv_sems.at[at], peer)
        for at, peer in enumerate(to)
    ]
    for copy in copies:
        copy.start()
    own = pltpu.make_async_copy(piece_of(flipped_ref, row, col), place_of(x_ref, row, col), own_sem)
    own.start()

    def step(at, carry):
        turned = lax.dot_general(
            w_bias_ref[0], normalize(pair_ref[at], gain_ref[0:1]), NT, preferred_element_type=jnp.float32
        )
        part[at] = turned[:HEADS].astype(jnp.bfloat16)
        return carry

    lax.fori_loop(0, part.shape[0], step, 0, unroll=4)
    gather_stages(size, part, full_ref, gather_send, gather_recv, gather_own)
    own.wait()
    for at, (dr, dc) in enumerate(shifts):
        source = lax.rem(row + rows - dr, rows)
        remote(
            piece_of(flipped_ref, row, col), place_of(x_ref, source, col), send_sems.at[at], recv_sems.at[at], to[at]
        ).wait_recv()
    for copy in copies:
        copy.wait_send()


def entry(pair, gain, w_bias, size):
    rows, cols = size
    deep, wide, channels = pair.shape
    width, count = wide // rows, deep * rows
    shifts = shifts_of(size, ("row",))
    part_shape = (deep, HEADS, wide)
    stages = cols - 1 + rows // 2
    return pl.pallas_call(
        functools.partial(
            entry_kernel,
            size,
            shifts,
            lambda ref, r, c: ref.at[pl.ds(r * width, width)],
            lambda ref, r, c: ref.at[:, pl.ds(pl.multiple_of(r * deep, deep), deep)],
        ),
        out_shape=[
            jax.ShapeDtypeStruct((width, count, channels), pair.dtype),
            jax.ShapeDtypeStruct((2, rows // 2, cols) + part_shape, pair.dtype),
        ],
        in_specs=[pl.BlockSpec(memory_space=pltpu.VMEM)] * 4,
        out_specs=[pl.BlockSpec(memory_space=pltpu.VMEM)] * 2,
        scratch_shapes=[
            pltpu.VMEM(part_shape, pair.dtype),
            pltpu.SemaphoreType.DMA((len(shifts),)),
            pltpu.SemaphoreType.DMA((len(shifts),)),
            pltpu.SemaphoreType.DMA,
            pltpu.SemaphoreType.DMA((stages,)),
            pltpu.SemaphoreType.DMA((stages,)),
            pltpu.SemaphoreType.DMA,
        ],
        compiler_params=pltpu.CompilerParams(collective_id=2, has_side_effects=True),
    )(pair, jnp.transpose(pair, (1, 0, 2)), gain, w_bias)


def local(pair, token_mask, gain, w_proj, w_bias, w_out, size):
    rows, cols = size
    deep, wide, channels = pair.shape
    width, count = wide // rows, deep * rows
    w_bias_turned = jnp.pad(jnp.transpose(w_bias, (0, 2, 1)), ((0, 0), (0, 16 - HEADS), (0, 0)))
    x, full = entry(pair, gain, w_bias_turned, size)
    turned = jnp.transpose(full, (4, 1, 0, 3, 2, 5)).reshape(HEADS, count, count)
    bias = finish_bias(turned, token_mask)
    if width % 2:
        x = attention(x, bias, gain[0], w_proj[0], w_out[0])
        x = swap(x, size)
        bias = gather_bias(x, token_mask, gain[1], w_bias[1], size)
    else:
        pairs = width // 2
        moved, full = fused(
            x,
            bias,
            gain,
            w_proj,
            w_bias_turned,
            w_out,
            0,
            (cols, rows, width, pairs, 2, channels),
            (width, count // 2, 2, channels),
            size,
            ("row", "col"),
            lambda ref, at, r, c: ref.at[at, pl.ds((r * cols + c) * pairs, pairs)],
            lambda ref, at, r, c: ref.at[c, r, at],
            3,
        )
        x = jnp.transpose(moved.reshape(count, width, channels), (1, 0, 2))
        turned = jnp.transpose(full, (4, 2, 1, 0, 3, 5)).reshape(HEADS, count, count)
        bias = finish_bias(turned, token_mask)
    return fused(
        x,
        bias,
        gain,
        w_proj,
        w_bias_turned,
        w_out,
        1,
        pair.shape,
        x.shape,
        size,
        ("col",),
        lambda ref, at, r, c: ref.at[at, pl.ds(pl.multiple_of(c * wide, wide), wide)],
        lambda ref, at, r, c: ref.at[pl.ds(c * width + at.start, at.size)],
        4,
    )[0]


def solution(mesh):
    size = (mesh.shape["row"], mesh.shape["col"])
    return jax.shard_map(
        functools.partial(local, size=size),
        mesh=mesh,
        in_specs=(P("row", "col", None), P(), P(), P(), P(), P()),
        out_specs=P("row", "col", None),
        check_vma=False,
    )
```

```python
import functools
import math

import jax
import jax.numpy as jnp
from jax import lax
from jax.experimental import pallas as pl
from jax.experimental.pallas import tpu as pltpu
from jax.sharding import PartitionSpec as P

HEADS = 4
HEAD_DIM = 32
INNER = HEADS * HEAD_DIM
LOG2E = 1.4426950408889634
LAG = 2
NT = (((1,), (1,)), ((), ()))
TN = (((0,), (0,)), ((), ()))


def normalize(tile, gain):
    values = tile.astype(jnp.float32)
    average = jnp.mean(values, axis=-1, keepdims=True)
    centred = values - average
    variance = jnp.mean(centred * centred, axis=-1, keepdims=True)
    return (centred * lax.rsqrt(variance + 1e-05) * gain).astype(jnp.bfloat16)


def attend(x, bias_ref, gain, w_turned_ref, w_k, w_out):
    count = x.shape[0]
    normed = normalize(x, gain)
    queries = lax.dot_general(w_turned_ref[:INNER], normed, NT, preferred_element_type=jnp.float32)
    rest = lax.dot_general(w_turned_ref[2 * INNER :], normed, NT, preferred_element_type=jnp.float32)
    keys = jnp.dot(normed, w_k, preferred_element_type=jnp.float32).astype(jnp.bfloat16)
    queries = (queries * (LOG2E / math.sqrt(HEAD_DIM))).astype(jnp.bfloat16)
    values = rest[:INNER].astype(jnp.bfloat16)
    gate = jax.nn.sigmoid(rest[INNER:])
    ones = jnp.ones((16, count), jnp.bfloat16)
    pieces = []
    for head in range(HEADS):
        low, high = head * HEAD_DIM, (head + 1) * HEAD_DIM
        parts = [queries[low:high]]
        if head:
            parts.insert(0, jnp.zeros((low, count), jnp.bfloat16))
        if head < HEADS - 1:
            parts.append(jnp.zeros((INNER - high, count), jnp.bfloat16))
        padded = jnp.concatenate(parts, axis=0)
        scores = jnp.dot(keys, padded, preferred_element_type=jnp.float32) + bias_ref[head]
        highest = jnp.max(scores, axis=0, keepdims=True)
        weights = jnp.exp2(scores - highest).astype(jnp.bfloat16)
        extended = jnp.concatenate([values[low:high], ones], axis=0)
        mixed = jnp.dot(extended, weights, preferred_element_type=jnp.float32)
        pieces.append(mixed[:HEAD_DIM] * (1.0 / mixed[HEAD_DIM : HEAD_DIM + 1]))
    gated = (gate * jnp.concatenate(pieces, axis=0)).astype(jnp.bfloat16)
    update = lax.dot_general(gated, w_out, TN, preferred_element_type=jnp.float32)
    return (x.astype(jnp.float32) + update).astype(jnp.bfloat16)


def attention_kernel(x_ref, bias_ref, gain_ref, w_turned_ref, w_k_ref, w_out_ref, out_ref):
    out_ref[0] = attend(x_ref[0], bias_ref, gain_ref[...], w_turned_ref, w_k_ref[...], w_out_ref[...])


def attention(x, bias, gain, w_proj, w_out):
    rows, count, channels = x.shape
    whole = lambda *shape: pl.BlockSpec(shape, lambda i: (0,) * len(shape))
    return pl.pallas_call(
        attention_kernel,
        out_shape=jax.ShapeDtypeStruct(x.shape, jnp.bfloat16),
        grid=(rows,),
        in_specs=[
            pl.BlockSpec((1, count, channels), lambda i: (i, 0, 0)),
            whole(HEADS, count, count),
            whole(1, channels),
            whole(4 * INNER, channels),
            whole(channels, INNER),
            whole(INNER, channels),
        ],
        out_specs=pl.BlockSpec((1, count, channels), lambda i: (i, 0, 0)),
    )(x, bias, gain[None], jnp.transpose(w_proj), w_proj[:, INNER : 2 * INNER], w_out)


def meet(peers):
    barrier = pltpu.get_barrier_semaphore()
    for peer in peers:
        pl.semaphore_signal(barrier, inc=1, device_id=peer, device_id_type=pl.DeviceIdType.MESH)
    pl.semaphore_wait(barrier, len(peers))


def remote(source, target, send_sem, recv_sem, peer):
    return pltpu.make_async_remote_copy(
        src_ref=source,
        dst_ref=target,
        send_sem=send_sem,
        recv_sem=recv_sem,
        device_id=peer,
        device_id_type=pl.DeviceIdType.MESH,
    )


def gather_peers(size):
    rows, cols = size
    row, col = lax.axis_index("row"), lax.axis_index("col")
    in_col = [(row, lax.rem(col + d, cols)) for d in range(1, cols)]
    in_row = [(lax.rem(row + 2 * d, rows), col) for d in range(1, rows // 2)]
    partner = (row // 2 * 2 + 1 - lax.rem(row, 2), col)
    return in_col, in_row, partner


def gather_stages(size, part_ref, full_ref, send_sems, recv_sems, own_sem, between=()):
    rows, cols = size
    row, col = lax.axis_index("row"), lax.axis_index("col")
    half, core = row // 2, lax.rem(row, 2)
    in_col, in_row, partner = gather_peers(size)
    sent = []

    def send(source, target, at, peer):
        copy = remote(source, target, send_sems.at[at], recv_sems.at[at], peer)
        copy.start()
        sent.append(copy)

    def arrive(target, at, peer):
        remote(target, target, send_sems.at[at], recv_sems.at[at], peer).wait_recv()

    mine = full_ref.at[core, half, col]
    for at, peer in enumerate(in_col):
        send(part_ref, mine, at, peer)
    own = pltpu.make_async_copy(part_ref, mine, own_sem)
    own.start()
    own.wait()
    for at, peer in enumerate(in_col):
        arrive(full_ref.at[core, half, lax.rem(col + cols - at - 1, cols)], at, peer)
    base = len(in_col)
    for at, peer in enumerate(in_row):
        send(full_ref.at[core, half], full_ref.at[core, half], base + at, peer)
    for copy in between:
        copy.start()
    halves = rows // 2
    for at, peer in enumerate(in_row):
        arrive(full_ref.at[core, lax.rem(half + halves - at - 1, halves)], base + at, peer)
    base += len(in_row)
    send(full_ref.at[core], full_ref.at[core], base, partner)
    arrive(full_ref.at[1 - core], base, partner)
    for copy in sent:
        copy.wait_send()


def gather_kernel(size, part_ref, full_ref, send_sems, recv_sems, own_sem):
    in_col, in_row, partner = gather_peers(size)
    meet(in_col + in_row + [partner])
    gather_stages(size, part_ref, full_ref, send_sems, recv_sems, own_sem)


def gather_steps(size, part, full_ref, send_sems, recv_sems, own_sems):
    rows, cols = size
    row, col = lax.axis_index("row"), lax.axis_index("col")
    half, core, halves = row // 2, lax.rem(row, 2), rows // 2
    in_col, in_row, partner = gather_peers(size)
    base = len(in_col)
    last = base + len(in_row)

    def link(source, target, at, index, peer):
        return remote(source, target, send_sems.at[at, index], recv_sems.at[at, index], peer)

    def own(at):
        return pltpu.make_async_copy(part.at[at], full_ref.at[core, half, col, at], own_sems.at[at])

    def to_col(at):
        mine = full_ref.at[core, half, col, at]
        return [link(part.at[at], mine, at, index, peer) for index, peer in enumerate(in_col)]

    def to_row(at):
        line = full_ref.at[core, half, :, at]
        return [link(line, line, at, base + index, peer) for index, peer in enumerate(in_row)]

    def to_partner(at):
        plane = full_ref.at[core, :, :, at]
        return link(plane, plane, at, last, partner)

    def send_part(at):
        own(at).start()
        for copy in to_col(at):
            copy.start()

    def pass_on(at):
        own(at).wait()
        for index, peer in enumerate(in_col):
            place = full_ref.at[core, half, lax.rem(col + cols - index - 1, cols), at]
            link(place, place, at, index, peer).wait_recv()
        for copy in to_row(at):
            copy.start()

    def share(at):
        for index, peer in enumerate(in_row):
            line = full_ref.at[core, lax.rem(half + halves - index - 1, halves), :, at]
            link(line, line, at, base + index, peer).wait_recv()
        to_partner(at).start()

    def finish(at, carry):
        plane = full_ref.at[1 - core, :, :, at]
        link(plane, plane, at, last, partner).wait_recv()
        for copy in to_col(at) + to_row(at) + [to_partner(at)]:
            copy.wait_send()
        return carry

    return send_part, pass_on, share, finish


def assemble(first_ref, mask_ref, bias_ref):
    cores, halves, cols, heads, deep, wide = first_ref.shape
    for half in range(halves):
        for core in range(cores):
            place = pl.ds((half * cores + core) * deep, deep)
            live = mask_ref[place] > 0
            for head in range(heads):
                pieces = [first_ref[core, half, col, head].astype(jnp.float32) for col in range(cols)]
                block = jnp.concatenate(pieces, axis=1) * LOG2E
                bias_ref[head, place, :] = jnp.where(live, block, -1000000000.0)


def fused_kernel(
    size, shifts, piece_of, place_of, turn, x_ref, gain_ref, w_proj_ref, w_bias_ref, w_out_ref, *rest
):
    bias_too = turn == 0
    group = 2 if bias_too else 1
    if bias_too:
        first_ref, mask_ref, out_ref, full_ref, stage, turned_ref, send_sems, recv_sems, own_sem = rest[:9]
        bias_ref, part, gather_send, gather_recv, gather_own = rest[9:]
    else:
        bias_ref, out_ref, stage, turned_ref, send_sems, recv_sems, own_sem = rest
    width = x_ref.shape[0]
    rows, cols = size
    row, col = lax.axis_index("row"), lax.axis_index("col")
    to = [(lax.rem(row + dr, rows), lax.rem(col + dc, cols)) for dr, dc in shifts]
    meet(to)
    turned_ref[...] = jnp.transpose(w_proj_ref[turn].astype(jnp.float32)).astype(jnp.bfloat16)

    def push(at):
        one = pl.ds(at, group)
        for index, peer in enumerate(to):
            remote(
                piece_of(stage, one, *peer),
                place_of(out_ref, one, row, col),
                send_sems.at[index],
                recv_sems.at[index],
                peer,
            ).start()
        pltpu.make_async_copy(piece_of(stage, one, row, col), place_of(out_ref, one, row, col), own_sem).start()

    if bias_too:
        assemble(first_ref, mask_ref, bias_ref)
        send_part, pass_on, share, finish = gather_steps(size, part, full_ref, gather_send, gather_recv, gather_own)

    def compute(at):
        result = attend(
            x_ref[at],
            bias_ref,
            gain_ref[turn : turn + 1],
            turned_ref,
            w_proj_ref[turn, :, INNER : 2 * INNER],
            w_out_ref[turn],
        )
        stage[at] = result.reshape(stage.shape[1:])
        if bias_too:
            turned = lax.dot_general(
                w_bias_ref[1], normalize(result, gain_ref[1:2]), NT, preferred_element_type=jnp.float32
            )
            part[at] = turned[:HEADS].astype(jnp.bfloat16)

    def step(at, carry):
        actions = []
        if bias_too:
            actions = [(1, send_part), (1 + LAG, pass_on), (1 + 2 * LAG, share)]
        @pl.when((at >= group) & (at <= width) & (lax.rem(at, group) == 0))
        def _():
            push(at - group)

        for delay, action in actions:

            @pl.when((at >= delay) & (at < width + delay))
            def _():
                action(at - delay)

        @pl.when(at < width)
        def _():
            compute(at)

        return carry

    lax.fori_loop(0, width + 1 + (2 * LAG if bias_too else 0), step, 0)
    if bias_too:
        lax.fori_loop(0, width, finish, 0)
    every = pl.ds(0, width)
    mine = piece_of(stage, every, row, col)
    pltpu.make_async_copy(mine, place_of(out_ref, every, row, col), own_sem).wait()
    for index, (dr, dc) in enumerate(shifts):
        source = (lax.rem(row + rows - dr, rows), lax.rem(col + cols - dc, cols))
        remote(
            mine, place_of(out_ref, every, *source), send_sems.at[index], recv_sems.at[index], to[index]
        ).wait_recv()
    for index, peer in enumerate(to):
        remote(
            piece_of(stage, every, *peer), place_of(out_ref, every, row, col), send_sems.at[index], recv_sems.at[index], peer
        ).wait_send()


def shifts_of(size, axes):
    return [
        (dr, dc)
        for dc in (range(size[1]) if "col" in axes else (0,))
        for dr in (range(size[0]) if "row" in axes else (0,))
        if dr or dc
    ]


def fused(x, bias, gain, w_proj, w_bias, w_out, turn, out_shape, stage_shape, size, axes, piece_of, place_of, collective_id):
    shifts = shifts_of(size, axes)
    operands = [x, gain, w_proj, w_bias, w_out, *bias]
    outs = [jax.ShapeDtypeStruct(out_shape, x.dtype)]
    scratch = [
        pltpu.VMEM(stage_shape, x.dtype),
        pltpu.VMEM((w_proj.shape[2], w_proj.shape[1]), x.dtype),
        pltpu.SemaphoreType.DMA((len(shifts),)),
        pltpu.SemaphoreType.DMA((len(shifts),)),
        pltpu.SemaphoreType.DMA,
    ]
    if turn == 0:
        part_shape = (x.shape[0], HEADS, x.shape[1])
        outs.append(jax.ShapeDtypeStruct((2, size[0] // 2, size[1]) + part_shape, x.dtype))
        count = size[1] - 1 + size[0] // 2
        scratch += [
            pltpu.VMEM((HEADS, x.shape[1], x.shape[1]), jnp.float32),
            pltpu.VMEM(part_shape, x.dtype),
            pltpu.SemaphoreType.DMA((x.shape[0], count)),
            pltpu.SemaphoreType.DMA((x.shape[0], count)),
            pltpu.SemaphoreType.DMA((x.shape[0],)),
        ]
    return pl.pallas_call(
        functools.partial(fused_kernel, size, shifts, piece_of, place_of, turn),
        out_shape=outs,
        in_specs=[pl.BlockSpec(memory_space=pltpu.VMEM)] * len(operands),
        out_specs=[pl.BlockSpec(memory_space=pltpu.VMEM)] * len(outs),
        scratch_shapes=scratch,
        compiler_params=pltpu.CompilerParams(collective_id=collective_id, has_side_effects=True),
    )(*operands)


def gather(part, size, collective_id):
    count = size[1] - 1 + size[0] // 2 - 1 + 1
    return pl.pallas_call(
        functools.partial(gather_kernel, size),
        out_shape=jax.ShapeDtypeStruct((2, size[0] // 2, size[1]) + part.shape, part.dtype),
        in_specs=[pl.BlockSpec(memory_space=pltpu.VMEM)],
        out_specs=pl.BlockSpec(memory_space=pltpu.VMEM),
        scratch_shapes=[
            pltpu.SemaphoreType.DMA((count,)),
            pltpu.SemaphoreType.DMA((count,)),
            pltpu.SemaphoreType.DMA,
        ],
        compiler_params=pltpu.CompilerParams(collective_id=collective_id, has_side_effects=True),
    )(part)


def gather_bias(x, token_mask, gain, w_bias, size):
    rows, count, channels = x.shape
    normed = normalize(x, gain)
    part = jnp.einsum("ikc,ch->ihk", normed, w_bias, preferred_element_type=jnp.float32)
    full = gather(part.astype(jnp.bfloat16), size, 1)
    turned = jnp.transpose(full, (4, 5, 1, 0, 2, 3)).reshape(HEADS, count, count)
    return finish_bias(turned, token_mask)


def finish_bias(turned, token_mask):
    return jnp.where(token_mask[None, :, None] > 0, turned.astype(jnp.float32) * LOG2E, -1000000000.0)


def swap(x, size):
    width, count, channels = x.shape
    rows, cols = size
    x = lax.all_to_all(x, "row", 1, 0, tiled=True)
    return lax.all_to_all(jnp.transpose(x, (1, 0, 2)), "col", 0, 1, tiled=True)


def entry_kernel(
    size, shifts, piece_of, place_of, pair_ref, flipped_ref, gain_ref, w_bias_ref, x_ref, full_ref, part, wide_part,
    send_sems, recv_sems, own_sem, gather_send, gather_recv, gather_own
):
    rows, cols = size
    row, col = lax.axis_index("row"), lax.axis_index("col")
    to = [(lax.rem(row + dr, rows), col) for dr, dc in shifts]
    in_col, in_row, partner = gather_peers(size)
    meet(to + in_col)
    copies = [
        remote(piece_of(flipped_ref, *peer), place_of(x_ref, row, col), send_sems.at[at], recv_sems.at[at], peer)
        for at, peer in enumerate(to)
    ]
    early = len(copies) // 2
    for copy in copies[:early]:
        copy.start()
    own = pltpu.make_async_copy(piece_of(flipped_ref, row, col), place_of(x_ref, row, col), own_sem)
    own.start()

    def step(at, carry):
        turned = lax.dot_general(
            w_bias_ref[0], normalize(pair_ref[at], gain_ref[0:1]), NT, preferred_element_type=jnp.float32
        )
        wide_part[at] = turned[:HEADS]
        return carry

    lax.fori_loop(0, pair_ref.shape[0], step, 0, unroll=4)
    for head in range(HEADS):
        part[head] = wide_part[:, head, :].astype(jnp.bfloat16)
    gather_stages(size, part, full_ref, gather_send, gather_recv, gather_own, copies[early:])
    own.wait()
    for at, (dr, dc) in enumerate(shifts):
        source = lax.rem(row + rows - dr, rows)
        remote(
            piece_of(flipped_ref, row, col), place_of(x_ref, source, col), send_sems.at[at], recv_sems.at[at], to[at]
        ).wait_recv()
    for copy in copies:
        copy.wait_send()


def entry(pair, gain, w_bias, size):
    rows, cols = size
    deep, wide, channels = pair.shape
    width, count = wide // rows, deep * rows
    shifts = shifts_of(size, ("row",))
    part_shape = (HEADS, deep, wide)
    stages = cols - 1 + rows // 2
    return pl.pallas_call(
        functools.partial(
            entry_kernel,
            size,
            shifts,
            lambda ref, r, c: ref.at[pl.ds(r * width, width)],
            lambda ref, r, c: ref.at[:, pl.ds(pl.multiple_of(r * deep, deep), deep)],
        ),
        out_shape=[
            jax.ShapeDtypeStruct((width, count, channels), pair.dtype),
            jax.ShapeDtypeStruct((2, rows // 2, cols) + part_shape, pair.dtype),
        ],
        in_specs=[pl.BlockSpec(memory_space=pltpu.VMEM)] * 4,
        out_specs=[pl.BlockSpec(memory_space=pltpu.VMEM)] * 2,
        scratch_shapes=[
            pltpu.VMEM(part_shape, pair.dtype),
            pltpu.VMEM((deep, HEADS, wide), jnp.float32),
            pltpu.SemaphoreType.DMA((len(shifts),)),
            pltpu.SemaphoreType.DMA((len(shifts),)),
            pltpu.SemaphoreType.DMA,
            pltpu.SemaphoreType.DMA((stages,)),
            pltpu.SemaphoreType.DMA((stages,)),
            pltpu.SemaphoreType.DMA,
        ],
        compiler_params=pltpu.CompilerParams(collective_id=2, has_side_effects=True),
    )(pair, jnp.transpose(pair, (1, 0, 2)), gain, w_bias)


def local(pair, token_mask, gain, w_proj, w_bias, w_out, size):
    rows, cols = size
    deep, wide, channels = pair.shape
    width, count = wide // rows, deep * rows
    w_bias_turned = jnp.pad(jnp.transpose(w_bias, (0, 2, 1)), ((0, 0), (0, 16 - HEADS), (0, 0)))
    x, full = entry(pair, gain, w_bias_turned, size)
    if width % 2:
        turned = jnp.transpose(full, (3, 1, 0, 4, 2, 5)).reshape(HEADS, count, count)
        bias = finish_bias(turned, token_mask)
        x = attention(x, bias, gain[0], w_proj[0], w_out[0])
        x = swap(x, size)
        bias = gather_bias(x, token_mask, gain[1], w_bias[1], size)
    else:
        pairs = width // 2
        moved, full = fused(
            x,
            (full, token_mask.reshape(count, 1)),
            gain,
            w_proj,
            w_bias_turned,
            w_out,
            0,
            (cols, rows, width, pairs, 2, channels),
            (width, count // 2, 2, channels),
            size,
            ("row", "col"),
            lambda ref, at, r, c: ref.at[at, pl.ds((r * cols + c) * pairs, pairs)],
            lambda ref, at, r, c: ref.at[c, r, at],
            3,
        )
        x = jnp.transpose(moved.reshape(count, width, channels), (1, 0, 2))
        turned = jnp.transpose(full, (4, 2, 1, 0, 3, 5)).reshape(HEADS, count, count)
        bias = finish_bias(turned, token_mask)
    return fused(
        x,
        (bias,),
        gain,
        w_proj,
        w_bias_turned,
        w_out,
        1,
        pair.shape,
        x.shape,
        size,
        ("col",),
        lambda ref, at, r, c: ref.at[at, pl.ds(pl.multiple_of(c * wide, wide), wide)],
        lambda ref, at, r, c: ref.at[pl.ds(c * width + at.start, at.size)],
        4,
    )[0]


def solution(mesh):
    size = (mesh.shape["row"], mesh.shape["col"])
    return jax.shard_map(
        functools.partial(local, size=size),
        mesh=mesh,
        in_specs=(P("row", "col", None), P(), P(), P(), P(), P()),
        out_specs=P("row", "col", None),
        check_vma=False,
    )
```
